32 devices in a mesh: groups: 2 (over y), ctx: 4 (over z), mp: 4 (over x, core).
Axes of the slice: x: 2, y: 2, z: 4, core: 2. Of those that a mesh axis runs over, the one named last changes fastest.
Arguments:
- query: bfloat16 [4096, 8192], P(('groups', 'ctx'), 'mp'), parts along dimension 0, may hold values from -200 to 200
- span_keys: bfloat16 [4096, 1024], P(('groups', 'ctx'), 'mp'), parts along dimension 0, may hold values from -6 to 6
- span_values: bfloat16 [4096, 1024], P(('groups', 'ctx'), 'mp'), parts along dimension 0, may hold values from -6 to 6
- cache_keys: bfloat16 [8192, 1024], P(('groups', 'ctx'), 'mp'), parts along dimension 0, may hold values from -13 to 13
- stored_values: bfloat16 [8192, 1024], P(('groups', 'ctx'), 'mp'), parts along dimension 0, may hold values from -6 to 6
- selected: int32 [8, 8, 2], P(('groups', 'ctx'), 'mp'), parts along dimension 0, may hold values from 0 to 7, as said below
Outputs:
- attended: bfloat16 [4096, 8192], P(('groups', 'ctx'), 'mp'), parts along dimension 0
The draws below stay inside these ranges and needn't reach their ends.
There are 2 independent parts, one for each index of `groups`. The reference program is written for one: setup_inputs(seed, part) draws one part's arguments, and reference() takes and returns one part's arrays. A program takes and returns all parts, laid end to end along the dimension named above; each array names one. Nothing has to cross between parts.
Inputs may be any that keep to these rules, and one draw needn't show every extreme that they name: `selected`: the two blocks chosen for a query block and key head lie in different ranges of 2 consecutive blocks, starting at multiples of 2.
All inputs are finite; a program needn't handle non-finite values.
Results may differ from the reference program's by a relative error of at most 0.0047.
Values may be sent and summed in bfloat16 or wider, within the bound.
No kernel may reach another device: no remote copies, remote signals or barrier semaphores. Data moves between devices by JAX's collectives and lax.ppermute only.
A program may use at most 64 MiB of HBM per device.

```python
import jax
import jax.numpy as jnp
from jax import lax

QUERY_HEADS = 64
KEY_VALUE_HEADS = 8
HEAD_DIMENSION = 128
BLOCK = 512
BLOCKS_PER_OWNER = 2
QUERY_BLOCKS = 4
SPAN_POSITIONS = 2048
CACHED_POSITIONS = 4096


def draw_query(key, part):
    regular_portion = jnp.clip(jax.random.normal(key, (SPAN_POSITIONS, QUERY_HEADS * HEAD_DIMENSION), jnp.float32), -6.0, 6.0)
    return regular_portion.astype(jnp.bfloat16)


def draw_cache_keys(key, part):
    regular_portion = jnp.clip(jax.random.normal(key, (CACHED_POSITIONS, KEY_VALUE_HEADS * HEAD_DIMENSION), jnp.float32), -6.0, 6.0)
    return regular_portion.astype(jnp.bfloat16)


def draw_selected(key, part):
    holder_count = CACHED_POSITIONS // (BLOCK * BLOCKS_PER_OWNER)
    leading_key, trailing_key, nested_key = jax.random.split(key, 3)
    leading_holder = jax.random.randint(leading_key, (QUERY_BLOCKS, KEY_VALUE_HEADS), 0, holder_count)
    trailing_holder = (leading_holder + jax.random.randint(trailing_key, (QUERY_BLOCKS, KEY_VALUE_HEADS), 1, holder_count)) % holder_count
    nested_block = jax.random.randint(nested_key, (QUERY_BLOCKS, KEY_VALUE_HEADS, 2), 0, BLOCKS_PER_OWNER)
    return (jnp.stack([leading_holder, trailing_holder], axis=-1) * BLOCKS_PER_OWNER + nested_block).astype(jnp.int32)


def block_scale(rng, extent, cuts, smallest, largest):
    loudness = 1.0
    for axis_at, blocks in cuts:
        heights = jax.random.uniform(jax.random.fold_in(jax.random.fold_in(rng, 6), axis_at), (blocks,), jnp.float32, smallest / len(cuts), largest / len(cuts))
        loudness = loudness * jnp.repeat(jnp.exp(heights), extent[axis_at] // blocks).reshape((-1,) + (1,) * (len(extent) - 1 - axis_at))
    return loudness


def gaussian(rng, shape, deviation, most, shards=(), kind=jnp.bfloat16):
    loudness = block_scale(rng, shape, shards, -0.22, 0.18) if shards else 1.0
    entries = jax.random.normal(rng, shape, jnp.float32) * deviation * loudness
    return jnp.minimum(jnp.maximum(entries, -most), most).astype(kind)


def setup_inputs(seed: int = 0, part: int = 0) -> dict:
    streams_of = jax.random.split(jax.random.key(seed), 7)
    own_keys = jax.random.split(jax.random.fold_in(streams_of[6], part), 7)
    return {
        "query": draw_query(jax.random.fold_in(jax.random.fold_in(streams_of[6], part), 71), part),
        "span_keys": gaussian(own_keys[1], (SPAN_POSITIONS, KEY_VALUE_HEADS * HEAD_DIMENSION), 1.0, 6.0, ((0, 4), (1, 4))),
        "span_values": gaussian(own_keys[2], (SPAN_POSITIONS, KEY_VALUE_HEADS * HEAD_DIMENSION), 1.0, 6.0, ((0, 4), (1, 4))),
        "cache_keys": draw_cache_keys(jax.random.fold_in(jax.random.fold_in(streams_of[6], part), 71), part),
        "stored_values": gaussian(own_keys[4], (CACHED_POSITIONS, KEY_VALUE_HEADS * HEAD_DIMENSION), 1.0, 6.0, ((0, 4), (1, 4))),
        "selected": draw_selected(jax.random.fold_in(jax.random.fold_in(streams_of[6], part), 71), part),
    }


def attend(query_group, all_keys, all_values, query_group_count):
    block_rows = query_group.shape[0]
    head_size = all_keys.shape[1]
    score_scale = head_size ** -0.5
    query_pos = jnp.arange(block_rows, dtype=jnp.int32)[:, None]
    key_pos = jnp.arange(all_keys.shape[0], dtype=jnp.int32)[None, :]
    visible = (key_pos >= block_rows) | (key_pos <= query_pos)
    results = []
    for member in range(query_group_count):
        query_head = query_group[:, member * head_size:(member + 1) * head_size]
        scores = jnp.dot(query_head, all_keys.T, preferred_element_type=jnp.float32) * score_scale
        scores = jnp.where(visible, scores, jnp.float32(-1e30))
        maxima = jnp.max(scores, axis=1, keepdims=True)
        exponent = jnp.exp(scores - maxima)
        denominator = jnp.sum(exponent, axis=1, keepdims=True)
        weights = (exponent / denominator).astype(jnp.bfloat16)
        results.append(jnp.dot(weights, all_values, preferred_element_type=jnp.float32).astype(jnp.bfloat16))
    return jnp.concatenate(results, axis=1)


def reference(query, span_keys, span_values, cache_keys, stored_values, selected):
    query_group_count = QUERY_HEADS // KEY_VALUE_HEADS

    def one_block(block_index):
        begin_row = (block_index * BLOCK).astype(jnp.int32)
        results = []
        for key_value_head in range(KEY_VALUE_HEADS):
            query_group = lax.dynamic_slice(query, (begin_row, jnp.int32(key_value_head * query_group_count * HEAD_DIMENSION)), (BLOCK, query_group_count * HEAD_DIMENSION))
            key_list = [lax.dynamic_slice(span_keys, (begin_row, jnp.int32(key_value_head * HEAD_DIMENSION)), (BLOCK, HEAD_DIMENSION))]
            value_list = [lax.dynamic_slice(span_values, (begin_row, jnp.int32(key_value_head * HEAD_DIMENSION)), (BLOCK, HEAD_DIMENSION))]
            for slot_index in range(2):
                first_row = (selected[block_index, key_value_head, slot_index] * BLOCK).astype(jnp.int32)
                key_list.append(lax.dynamic_slice(cache_keys, (first_row, jnp.int32(key_value_head * HEAD_DIMENSION)), (BLOCK, HEAD_DIMENSION)))
                value_list.append(lax.dynamic_slice(stored_values, (first_row, jnp.int32(key_value_head * HEAD_DIMENSION)), (BLOCK, HEAD_DIMENSION)))
            results.append(attend(query_group, jnp.concatenate(key_list, axis=0), jnp.concatenate(value_list, axis=0), query_group_count))
        return jnp.concatenate(results, axis=1)

    blocks_out = lax.map(one_block, jnp.arange(QUERY_BLOCKS, dtype=jnp.int32))
    return blocks_out.reshape(SPAN_POSITIONS, QUERY_HEADS * HEAD_DIMENSION)
```

```python
import jax
import jax.numpy as jnp
from jax import lax
from jax.experimental import pallas as pl
from jax.experimental.pallas import tpu as pltpu
from jax.sharding import PartitionSpec as P

HEAD = 128
LOG2E = 1.4426950408889634
NEG = -1e30
VMEM = pl.BlockSpec(memory_space=pltpu.VMEM)
ANY = pl.BlockSpec(memory_space=pl.ANY)
SMEM = pl.BlockSpec(memory_space=pltpu.SMEM)
PARAMS = pltpu.CompilerParams(vmem_limit_bytes=8 << 20)


def near_core(x):
    return pltpu.with_memory_space_constraint(x, pltpu.VMEM)


def local_row(sel, owner, h, per_owner):
    a, b = sel[0, h, 0], sel[0, h, 1]
    lo = owner * per_owner
    in_a = (a >= lo) & (a < lo + per_owner)
    in_b = (b >= lo) & (b < lo + per_owner)
    return jnp.where(in_a, a - lo, jnp.where(in_b, b - lo, 0))


def wants(sel, owner, h, per_owner):
    a, b = sel[0, h, 0], sel[0, h, 1]
    lo = owner * per_owner
    return ((a >= lo) & (a < lo + per_owner)) | ((b >= lo) & (b < lo + per_owner))


def with_ones(v):
    return jnp.concatenate([v, jnp.ones((v.shape[0], HEAD), jnp.bfloat16)], axis=1)


def scores_of(q, k):
    return lax.dot_general(q, k, (((1,), (1,)), ((), ())), preferred_element_type=jnp.float32)


SCALE = LOG2E * HEAD ** -0.5


def own_tile(q, k, v, first_key):
    s = scores_of(q, k)
    half = q.shape[0]
    qpos = lax.broadcasted_iota(jnp.int32, (half, half), 0)
    kpos = lax.broadcasted_iota(jnp.int32, (half, half), 1)
    tail = jnp.where(kpos <= qpos, s[:, first_key:], NEG)
    s = jnp.concatenate([s[:, :first_key], tail], axis=1) if first_key else tail
    top = jnp.max(s, axis=1, keepdims=True)
    p = jnp.exp2((s - top) * SCALE).astype(jnp.bfloat16)
    sums = jnp.dot(p, v, preferred_element_type=jnp.float32)
    return sums[:, :HEAD], sums[:, HEAD:], jnp.broadcast_to(top, (half, HEAD))


def chunk_tile(q, k, v, acc, den, old):
    s = scores_of(q, k)
    top = jnp.maximum(old, jnp.max(s, axis=1, keepdims=True))
    p = jnp.concatenate(
        [jnp.exp2((s[:, j:j + HEAD] - top) * SCALE) for j in range(0, s.shape[1], HEAD)], axis=1).astype(jnp.bfloat16)
    sums = jnp.dot(p, v, preferred_element_type=jnp.float32)
    keep = jnp.exp2((old - top) * SCALE)
    return acc * keep + sums[:, :HEAD], den * keep + sums[:, HEAD:], top


def cell(r, half, head):
    return pl.ds(r * half, half), pl.ds(pl.multiple_of(head * HEAD, HEAD), HEAD)


def state_shapes(query):
    return [pltpu.VMEM(query.shape, jnp.float32)] * 3


def cost(rows, heads, blocks):
    work = rows * rows * heads * blocks
    return pl.CostEstimate(flops=4 * work * HEAD, transcendentals=work, bytes_accessed=rows * heads * HEAD * 16)


STEP = 2


def add_chunk(q_ref, before, state, kv, h, group, half):
    k, v = kv
    v = with_ones(v)

    def step(g, carry):
        for i in range(STEP):
            head = h * group + g * STEP + i
            for r in range(2):
                at = cell(r, half, head)
                acc, den, top = chunk_tile(q_ref[at], k, v, before[0][at], before[1][at], before[2][at])
                state[0][at] = acc
                state[1][at] = den
                state[2][at] = top
        return carry

    lax.fori_loop(0, group // STEP, step, 0)


def own_and_local(me, sel, query, span_keys, span_values, keys, values, per_owner, group):
    rows, half = query.shape[0], query.shape[0] // 2
    kv_heads = span_keys.shape[1] // HEAD

    def body(me_ref, sel_ref, q_ref, sk_ref, sv_ref, k_ref, v_ref, *state):
        for h in range(kv_heads):
            col = slice(h * HEAD, (h + 1) * HEAD)
            own_k, own_v = sk_ref[:, col], with_ones(sv_ref[:, col])

            def step(g, carry):
                for i in range(STEP):
                    head = h * group + g * STEP + i
                    for r in range(2):
                        at = cell(r, half, head)
                        n = (r + 1) * half
                        acc, den, top = own_tile(q_ref[at], own_k[:n], own_v[:n], r * half)
                        state[0][at] = acc
                        state[1][at] = den
                        state[2][at] = top
                return carry

            lax.fori_loop(0, group // STEP, step, 0)
            if per_owner:
                @pl.when(wants(sel_ref, me_ref[0], h, per_owner))
                def _():
                    at = pl.ds(pl.multiple_of(local_row(sel_ref, me_ref[0], h, per_owner) * rows, rows), rows)
                    add_chunk(q_ref, state, state, (k_ref[at, col], v_ref[at, col]), h, group, half)

    return pl.pallas_call(
        body, out_shape=state_shapes(query), in_specs=[SMEM] * 2 + [VMEM] * 5, out_specs=[VMEM] * 3,
        compiler_params=PARAMS, cost_estimate=cost(rows, kv_heads * group, 2),
    )(me, sel, *map(near_core, (query, span_keys, span_values, keys, values)))


def more_chunks(me, sel, query, sources, state, group, kv_heads, blocks):
    rows, half = query.shape[0], query.shape[0] // 2
    arrays = [a for s in sources for a in s[0]]

    def body(me_ref, sel_ref, q_ref, *refs):
        refs, old, state = refs[:len(arrays)], refs[len(arrays):len(arrays) + 3], refs[len(arrays) + 3:]
        for h in range(kv_heads):
            cols = slice(h * group * HEAD, (h + 1) * group * HEAD)
            at = 0
            for i, source in enumerate(sources):
                mine = refs[at:at + len(source[0])]
                at += len(source[0])
                needed = source[1](me_ref[0], sel_ref, h)

                @pl.when(needed)
                def _():
                    kv = source[2](mine, me_ref[0], sel_ref, h)
                    add_chunk(q_ref, state if i else old, state, kv, h, group, half)

                if i == 0:
                    @pl.when(jnp.logical_not(needed))
                    def _():
                        for new, previous in zip(state, old):
                            new[:, cols] = previous[:, cols]

    n = 3 + len(arrays)
    return pl.pallas_call(
        body, out_shape=state_shapes(query), in_specs=[SMEM] * 2 + [VMEM] * (n + 1), out_specs=[VMEM] * 3,
        compiler_params=PARAMS, cost_estimate=cost(rows, kv_heads * group, blocks),
    )(me, sel, *map(near_core, (query, *arrays, *state)))


def finish(me, sel, query, arrays, when, read, state, group, head, out):
    rows, half = query.shape[0], query.shape[0] // 2
    wide = STEP * HEAD
    steps = group // STEP

    def body(me_ref, sel_ref, q_ref, *refs):
        refs, state, o_ref = refs[:len(arrays)], refs[len(arrays):len(arrays) + 3], refs[-1]
        g = pl.program_id(0)

        def tiles(fn):
            for i in range(STEP):
                for r in range(2):
                    at = cell(r, half, head * group + g * STEP + i)
                    acc, den = fn(at)
                    o_ref[r * half:(r + 1) * half, i * HEAD:(i + 1) * HEAD] = (acc / den).astype(jnp.bfloat16)

        needed = when(me_ref[0], sel_ref, head)

        @pl.when(needed)
        def _():
            k, v = read(refs, me_ref[0], sel_ref, head)
            v = with_ones(v)
            tiles(lambda at: chunk_tile(q_ref[at], k, v, state[0][at], state[1][at], state[2][at])[:2])

        @pl.when(jnp.logical_not(needed))
        def _():
            tiles(lambda at: (state[0][at], state[1][at]))

    extra = [] if out is None else [out]
    n = 6 + len(arrays)
    return pl.pallas_call(
        body, out_shape=jax.ShapeDtypeStruct(query.shape, jnp.bfloat16), grid=(steps,),
        in_specs=[SMEM] * 2 + [VMEM] * (n - 2) + [ANY] * len(extra),
        out_specs=pl.BlockSpec((rows, wide), lambda g: (0, head * steps + g)),
        input_output_aliases={n: 0} if extra else {},
        compiler_params=PARAMS, cost_estimate=cost(rows, group, 1),
    )(me, sel, *map(near_core, (query, *arrays, *state)), *extra)


def pick(me, sels, arrays, rows, jobs):
    n, k = len(sels), len(arrays)

    def body(me_ref, *refs):
        sel_refs, refs, outs = refs[:n], refs[n:n + k], refs[n + k:]
        for out, parts in zip(outs, jobs):
            for when, keys, values, row, h, place in parts:
                def copy():
                    at = pl.ds(pl.multiple_of(row(me_ref[0], sel_refs, h) * rows, rows), rows)
                    col = slice(h * HEAD, (h + 1) * HEAD)
                    out[2 * place * rows:(2 * place + 1) * rows] = refs[keys][at, col]
                    out[(2 * place + 1) * rows:(2 * place + 2) * rows] = refs[values][at, col]
                if when is None:
                    copy()
                else:
                    pl.when(when(me_ref[0]))(copy)

    shapes = [pltpu.VMEM((2 * rows * (1 + max(p[5] for p in parts)), HEAD), jnp.bfloat16) for parts in jobs]
    return pl.pallas_call(
        body, out_shape=shapes, in_specs=[SMEM] * (1 + n) + [VMEM] * k, out_specs=[VMEM] * len(jobs),
        compiler_params=PARAMS,
        cost_estimate=pl.CostEstimate(flops=0, transcendentals=0, bytes_accessed=8 * rows * HEAD * len(jobs)),
    )(me, *sels, *map(near_core, arrays))


def gathered(query, span_keys, span_values, cache_keys, stored_values, selected, group):
    rows = query.shape[0]
    kv_heads = span_keys.shape[1] // HEAD
    me = lax.axis_index("ctx").astype(jnp.int32).reshape(1)
    keys = lax.all_gather(cache_keys, "ctx", axis=0, tiled=True)
    values = lax.all_gather(stored_values, "ctx", axis=0, tiled=True)
    state = own_and_local(me, selected, query, span_keys, span_values, cache_keys, stored_values, 0, group)

    def always(m, s, h):
        return m >= 0

    def chosen(array, h, slot):
        start = jnp.clip(selected[0, h, slot], 0, keys.shape[0] // rows - 1) * rows
        return lax.dynamic_slice(array, (start, h * HEAD), (rows, HEAD))

    def whole(refs, m, s, h):
        return refs[2 * h][...], refs[2 * h + 1][...]

    blocks = [[chosen(a, h, slot) for h in range(kv_heads) for a in (keys, values)] for slot in range(2)]
    state = more_chunks(me, selected, query, [(blocks[0], always, whole)], state, group, kv_heads, 1)
    out = None
    for h in range(kv_heads):
        out = finish(me, selected, query, blocks[1], always, whole, state, group, h, out)
    return out


def line_of_four(query, span_keys, span_values, cache_keys, stored_values, selected, group):
    rows = query.shape[0]
    kv_heads = span_keys.shape[1] // HEAD
    per_owner = cache_keys.shape[0] // rows
    me = lax.axis_index("ctx").astype(jnp.int32).reshape(1)
    heads = range(kv_heads)

    def inner(m):
        return (m == 1) | (m == 2)

    def outer(m):
        return (m == 0) | (m == 3)

    sel1 = lax.ppermute(selected, "ctx", [(0, 1), (1, 0), (2, 3), (3, 2)])
    mid_keys = lax.ppermute(cache_keys, "ctx", [(1, 2), (2, 1)])
    mid_values = lax.ppermute(stored_values, "ctx", [(1, 2), (2, 1)])
    state = own_and_local(me, selected, query, span_keys, span_values, cache_keys, stored_values, per_owner, group)

    sel1, state = lax.optimization_barrier((sel1, state))
    both = lax.ppermute(jnp.concatenate([selected, sel1], axis=0), "ctx", [(3, 0), (0, 3)])
    near_out, = pick(
        me, (sel1,), (cache_keys, stored_values), rows,
        [[(None, 0, 1, lambda m, s, h: local_row(s[0], m, h, per_owner), h, h) for h in heads]])
    near = lax.ppermute(near_out, "ctx", [(0, 1), (1, 0), (2, 3), (3, 2)])
    sel3, sel2 = both[:1], both[1:]
    far_out = pick(
        me, (sel3,), (cache_keys, stored_values), rows,
        [[(outer, 0, 1, lambda m, s, h: local_row(s[0], m, h, per_owner), h, 0)] for h in heads])

    cross_out, = pick(
        me, (sel1, sel2), (cache_keys, stored_values, mid_keys, mid_values), rows,
        [[part for h in heads for part in (
            (inner, 2, 3, lambda m, s, h: local_row(s[0], m ^ 3, h, per_owner), h, h),
            (outer, 0, 1, lambda m, s, h: local_row(s[1], m, h, per_owner), h, h))]])
    cross = lax.ppermute(cross_out, "ctx", [(0, 2), (3, 1), (1, 0), (2, 3)])
    far = [lax.ppermute(f, "ctx", [(0, 3), (3, 0)]) for f in far_out]

    def stacked(refs, m, s, h):
        return refs[0][2 * h * rows:(2 * h + 1) * rows], refs[0][(2 * h + 1) * rows:(2 * h + 2) * rows]

    def middle(refs, m, s, h):
        at = pl.ds(pl.multiple_of(local_row(s, m ^ 3, h, per_owner) * rows, rows), rows)
        col = slice(h * HEAD, (h + 1) * HEAD)
        return refs[0][at, col], refs[1][at, col]

    def single(refs, m, s, h):
        return refs[0][:rows], refs[0][rows:]

    state = more_chunks(
        me, selected, query,
        [((near,), lambda m, s, h: wants(s, m ^ 1, h, per_owner), stacked),
         ((mid_keys, mid_values), lambda m, s, h: inner(m) & wants(s, m ^ 3, h, per_owner), middle)],
        state, group, kv_heads, 1)
    state = more_chunks(
        me, selected, query, [((cross,), lambda m, s, h: wants(s, m ^ 2, h, per_owner), stacked)],
        state, group, kv_heads, 1)
    out = None
    for h in heads:
        out = finish(me, selected, query, (far[h],), lambda m, s, h: outer(m) & wants(s, m ^ 3, h, per_owner),
                     single, state, group, h, out)
    return out


def solution(mesh):
    kv = P(("groups", "ctx"), "mp")
    plan = line_of_four if mesh.shape["ctx"] == 4 else gathered

    def per_device(query, span_keys, span_values, cache_keys, stored_values, selected):
        group = query.shape[1] // span_keys.shape[1]
        return plan(query, span_keys, span_values, cache_keys, stored_values, selected, group)

    return jax.shard_map(
        per_device, mesh=mesh, in_specs=(kv, kv, kv, kv, kv, P(("groups", "ctx"), "mp", None)),
        out_specs=kv, check_vma=False)
```

```python
import jax
import jax.numpy as jnp
from jax import lax
from jax.experimental import pallas as pl
from jax.experimental.pallas import tpu as pltpu
from jax.sharding import PartitionSpec as P

HEAD = 128
LOG2E = 1.4426950408889634
NEG = -1e30
VMEM = pl.BlockSpec(memory_space=pltpu.VMEM)
ANY = pl.BlockSpec(memory_space=pl.ANY)
SMEM = pl.BlockSpec(memory_space=pltpu.SMEM)
PARAMS = pltpu.CompilerParams(vmem_limit_bytes=8 << 20)
WIDE = pltpu.CompilerParams(vmem_limit_bytes=20 << 20)


def near_core(x):
    return pltpu.with_memory_space_constraint(x, pltpu.VMEM)


def in_hbm(x):
    return pltpu.with_memory_space_constraint(x, pltpu.HBM)


def local_row(sel, owner, h, per_owner, at=0):
    a, b = sel[at, h, 0], sel[at, h, 1]
    lo = owner * per_owner
    in_a = (a >= lo) & (a < lo + per_owner)
    in_b = (b >= lo) & (b < lo + per_owner)
    return jnp.where(in_a, a - lo, jnp.where(in_b, b - lo, 0))


def wants(sel, owner, h, per_owner):
    a, b = sel[0, h, 0], sel[0, h, 1]
    lo = owner * per_owner
    return ((a >= lo) & (a < lo + per_owner)) | ((b >= lo) & (b < lo + per_owner))


def with_ones(v):
    return jnp.concatenate([v, jnp.ones((v.shape[0], HEAD), jnp.bfloat16)], axis=1)


def scores_of(q, k):
    return lax.dot_general(q, k, (((1,), (1,)), ((), ())), preferred_element_type=jnp.float32)


SCALE = LOG2E * HEAD ** -0.5


def own_rest(s, v, mask, first_key):
    s = jnp.concatenate([s[:, :first_key], s[:, first_key:] + mask], axis=1) if first_key else s + mask
    top = jnp.max(s, axis=1, keepdims=True)
    p = jnp.exp2((s - top) * SCALE).astype(jnp.bfloat16)
    sums = jnp.dot(p, v, preferred_element_type=jnp.float32)
    return sums[:, :HEAD], sums[:, HEAD:], jnp.broadcast_to(top, (s.shape[0], HEAD))


def chunk_tile(q, k, v, acc, den, old):
    s = scores_of(q, k)
    top = jnp.maximum(old, jnp.max(s, axis=1, keepdims=True))
    p = jnp.concatenate(
        [jnp.exp2((s[:, j:j + HEAD] - top) * SCALE) for j in range(0, s.shape[1], HEAD)], axis=1).astype(jnp.bfloat16)
    sums = jnp.dot(p, v, preferred_element_type=jnp.float32)
    keep = jnp.exp2((old - top) * SCALE)
    return acc * keep + sums[:, :HEAD], den * keep + sums[:, HEAD:], top


def cell(r, tile, head):
    rows = slice(r * tile, (r + 1) * tile)
    if isinstance(head, int):
        return rows, slice(head * HEAD, (head + 1) * HEAD)
    return rows, pl.ds(pl.multiple_of(head * HEAD, HEAD), HEAD)


def column(h, width=HEAD):
    return slice(h * width, (h + 1) * width) if isinstance(h, int) else pl.ds(pl.multiple_of(h * width, width), width)


def state_shapes(query):
    return [pltpu.VMEM(query.shape, jnp.float32)] * 3


def cost(rows, heads, blocks):
    work = rows * rows * heads * blocks
    return pl.CostEstimate(flops=4 * work * HEAD, transcendentals=work, bytes_accessed=rows * heads * HEAD * 16)


def add_chunk(q_ref, before, state, kv, h, group, tile):
    k, v = kv
    v = with_ones(v)
    for i in range(group):
        for r in range(q_ref.shape[0] // tile):
            at = cell(r, tile, h * group + i)
            new = chunk_tile(q_ref[at], k, v, before[0][at], before[1][at], before[2][at])
            for ref, value in zip(state, new):
                ref[at] = value


def own_and_local(me, sel, query, span_keys, span_values, keys, values, per_owner, group):
    rows, half = query.shape[0], query.shape[0] // 2
    kv_heads = span_keys.shape[1] // HEAD

    def body(me_ref, sel_ref, q_ref, sk_ref, sv_ref, k_ref, v_ref, *refs):
        state, mask_ref = refs[:3], refs[3]
        qpos = lax.broadcasted_iota(jnp.int32, (half, half), 0)
        kpos = lax.broadcasted_iota(jnp.int32, (half, half), 1)
        mask_ref[...] = jnp.where(kpos <= qpos, 0.0, NEG)

        def one_head(h, carry):
            col = column(h)
            own_k, own_v = sk_ref[:, col], with_ones(sv_ref[:, col])
            work = [(r, cell(r, half, h * group + i)) for r in range(2) for i in range(group)]
            queries = [q_ref[at] for _, at in work]

            def scores(j):
                return scores_of(queries[j], own_k[:(work[j][0] + 1) * half])

            done, s = [], scores(0)
            for j, (r, at) in enumerate(work):
                following = scores(j + 1) if j + 1 < len(work) else None
                done.append(own_rest(s, own_v[:(r + 1) * half], mask_ref[...], r * half))
                s = following
            for (_, at), new in zip(work, done):
                for ref, value in zip(state, new):
                    ref[at] = value
            if per_owner:
                @pl.when(wants(sel_ref, me_ref[0], h, per_owner))
                def _():
                    at = pl.ds(pl.multiple_of(local_row(sel_ref, me_ref[0], h, per_owner) * rows, rows), rows)
                    add_chunk(q_ref, state, state, (k_ref[at, col], v_ref[at, col]), h, group, rows // 4)
            return carry

        lax.fori_loop(0, kv_heads, one_head, 0)

    return pl.pallas_call(
        body, out_shape=state_shapes(query), in_specs=[SMEM] * 2 + [VMEM] * 5, out_specs=[VMEM] * 3,
        scratch_shapes=[pltpu.VMEM((half, half), jnp.float32)],
        compiler_params=WIDE, cost_estimate=cost(rows, kv_heads * group, 2),
    )(me, sel, *map(in_hbm, (query, span_keys, span_values, keys, values)))


def more_chunks(me, sel, query, sources, state, group, kv_heads, blocks):
    rows, half = query.shape[0], query.shape[0] // 2
    arrays = [a for s in sources for a in s[0]]

    def body(me_ref, sel_ref, q_ref, *refs):
        refs, old, state = refs[:len(arrays)], refs[len(arrays):len(arrays) + 3], refs[len(arrays) + 3:]
        def one_head(h, carry):
            cols = column(h, group * HEAD)
            at = 0
            for i, source in enumerate(sources):
                mine = refs[at:at + len(source[0])]
                at += len(source[0])
                needed = source[1](me_ref[0], sel_ref, h)

                @pl.when(needed)
                def _():
                    kv = source[2](mine, me_ref[0], sel_ref, h)
                    add_chunk(q_ref, state if i else old, state, kv, h, group, rows // 4)

                if i == 0:
                    @pl.when(jnp.logical_not(needed))
                    def _():
                        for new, previous in zip(state, old):
                            new[:, cols] = previous[:, cols]
            return carry

        lax.fori_loop(0, kv_heads, one_head, 0)

    n = 3 + len(arrays)
    return pl.pallas_call(
        body, out_shape=state_shapes(query), in_specs=[SMEM] * 2 + [VMEM] * (n + 1), out_specs=[VMEM] * 3,
        compiler_params=PARAMS, cost_estimate=cost(rows, kv_heads * group, blocks),
    )(me, sel, *map(near_core, (query, *arrays, *state)))


def finish(me, sel, query, arrays, when, read, state, group, head, out):
    rows = query.shape[0]
    tile = rows // 4
    first = head * group

    def body(me_ref, sel_ref, q_ref, *refs):
        refs, state, (o_ref, buf, sem) = refs[:len(arrays)], refs[len(arrays):len(arrays) + 3], refs[-3:]

        def tiles(fn):
            copies = []
            for i in range(group):
                for r in range(rows // tile):
                    acc, den = fn(cell(r, tile, first + i))
                    buf[cell(r, tile, i)] = (acc / den).astype(jnp.bfloat16)
                copies.append(pltpu.make_async_copy(
                    buf.at[:, pl.ds(i * HEAD, HEAD)], o_ref.at[:, pl.ds((first + i) * HEAD, HEAD)], sem.at[i]))
                copies[-1].start()
            for copy in copies:
                copy.wait()

        needed = when(me_ref[0], sel_ref, head)

        @pl.when(needed)
        def _():
            k, v = read(refs, me_ref[0], sel_ref, head)
            v = with_ones(v)
            tiles(lambda at: chunk_tile(q_ref[at], k, v, state[0][at], state[1][at], state[2][at])[:2])

        @pl.when(jnp.logical_not(needed))
        def _():
            tiles(lambda at: (state[0][at], state[1][at]))

    extra = [] if out is None else [out]
    n = 6 + len(arrays)
    return pl.pallas_call(
        body, out_shape=jax.ShapeDtypeStruct(query.shape, jnp.bfloat16),
        in_specs=[SMEM] * 2 + [VMEM] * (n - 2) + [ANY] * len(extra), out_specs=ANY,
        scratch_shapes=[pltpu.VMEM((rows, group * HEAD), jnp.bfloat16), pltpu.SemaphoreType.DMA((group,))],
        input_output_aliases={n: 0} if extra else {},
        compiler_params=PARAMS, cost_estimate=cost(rows, group, 1),
    )(me, sel, *map(near_core, (query, *arrays, *state)), *extra)


def pick(me, sels, arrays, rows, jobs, place=near_core):
    n, k = len(sels), len(arrays)

    def body(me_ref, *refs):
        sel_refs, refs, outs = refs[:n], refs[n:n + k], refs[n + k:]
        for out, parts in zip(outs, jobs):
            for when, keys, values, row, h, slot in parts:
                def copy():
                    at = pl.ds(pl.multiple_of(row(me_ref[0], sel_refs, h) * rows, rows), rows)
                    col = slice(h * HEAD, (h + 1) * HEAD)
                    out[2 * slot * rows:(2 * slot + 1) * rows] = refs[keys][at, col]
                    out[(2 * slot + 1) * rows:(2 * slot + 2) * rows] = refs[values][at, col]
                if when is None:
                    copy()
                else:
                    pl.when(when(me_ref[0]))(copy)

    shapes = [pltpu.VMEM((2 * rows * (1 + max(p[5] for p in parts)), HEAD), jnp.bfloat16) for parts in jobs]
    return pl.pallas_call(
        body, out_shape=shapes, in_specs=[SMEM] * (1 + n) + [VMEM] * k, out_specs=[VMEM] * len(jobs),
        compiler_params=PARAMS,
        cost_estimate=pl.CostEstimate(flops=0, transcendentals=0, bytes_accessed=8 * rows * HEAD * len(jobs)),
    )(me, *sels, *map(place, arrays))


def gathered(query, span_keys, span_values, cache_keys, stored_values, selected, group):
    rows = query.shape[0]
    kv_heads = span_keys.shape[1] // HEAD
    me = lax.axis_index("ctx").astype(jnp.int32).reshape(1)
    keys = lax.all_gather(cache_keys, "ctx", axis=0, tiled=True)
    values = lax.all_gather(stored_values, "ctx", axis=0, tiled=True)
    state = own_and_local(me, selected, query, span_keys, span_values, cache_keys, stored_values, 0, group)

    def always(m, s, h):
        return m >= 0

    def chosen(array, h, slot):
        start = jnp.clip(selected[0, h, slot], 0, keys.shape[0] // rows - 1) * rows
        return lax.dynamic_slice(array, (start, h * HEAD), (rows, HEAD))

    def stacked(refs, m, s, h):
        start = pl.multiple_of(2 * h * rows, rows)
        return refs[0][pl.ds(start, rows)], refs[0][pl.ds(start + rows, rows)]

    blocks = [[jnp.concatenate([chosen(a, h, slot) for h in range(kv_heads) for a in (keys, values)])] for slot in range(2)]
    state = more_chunks(me, selected, query, [(blocks[0], always, stacked)], state, group, kv_heads, 1)
    out = None
    for h in range(kv_heads):
        out = finish(me, selected, query, blocks[1], always, stacked, state, group, h, out)
    return out


def line_of_four(query, span_keys, span_values, cache_keys, stored_values, selected, group):
    rows = query.shape[0]
    kv_heads = span_keys.shape[1] // HEAD
    per_owner = cache_keys.shape[0] // rows
    me = lax.axis_index("ctx").astype(jnp.int32).reshape(1)
    heads = range(kv_heads)

    def inner(m):
        return (m == 1) | (m == 2)

    def outer(m):
        return (m == 0) | (m == 3)

    sel1 = lax.ppermute(selected, "ctx", [(0, 1), (1, 0), (2, 3), (3, 2)])
    mid_keys = lax.ppermute(cache_keys, "ctx", [(1, 2), (2, 1)])
    mid_values = lax.ppermute(stored_values, "ctx", [(1, 2), (2, 1)])
    both = lax.ppermute(jnp.concatenate([selected, sel1], axis=0), "ctx", [(3, 0), (0, 3)])

    near_out, far_out = pick(
        me, (sel1, both), (cache_keys, stored_values), rows,
        [[(None, 0, 1, lambda m, s, h: local_row(s[0], m, h, per_owner), h, h) for h in heads],
         [(outer, 0, 1, lambda m, s, h: local_row(s[1], m, h, per_owner), h, h) for h in heads]], in_hbm)
    near = lax.ppermute(near_out, "ctx", [(0, 1), (1, 0), (2, 3), (3, 2)])
    far = lax.ppermute(far_out, "ctx", [(0, 3), (3, 0)])

    near_out, far_out, span_keys = lax.optimization_barrier((near_out, far_out, span_keys))
    state = own_and_local(me, selected, query, span_keys, span_values, cache_keys, stored_values, per_owner, group)

    mid_keys, mid_values, state = lax.optimization_barrier((mid_keys, mid_values, state))
    cross_out = pick(
        me, (sel1, both), (cache_keys, stored_values, mid_keys, mid_values), rows,
        [[(inner, 2, 3, lambda m, s, h: local_row(s[0], m ^ 3, h, per_owner), h, 0),
          (outer, 0, 1, lambda m, s, h: local_row(s[1], m, h, per_owner, 1), h, 0)] for h in heads])
    cross = [lax.ppermute(c, "ctx", [(0, 2), (3, 1), (1, 0), (2, 3)]) for c in cross_out]

    def stacked(refs, m, s, h):
        start = pl.multiple_of(2 * h * rows, rows)
        return refs[0][pl.ds(start, rows)], refs[0][pl.ds(start + rows, rows)]

    def middle(refs, m, s, h):
        at = pl.ds(pl.multiple_of(local_row(s, m ^ 3, h, per_owner) * rows, rows), rows)
        return refs[0][at, column(h)], refs[1][at, column(h)]

    def single(refs, m, s, h):
        return refs[0][:rows], refs[0][rows:]

    near, far, cross_out, state = lax.optimization_barrier((near, far, cross_out, state))
    state = more_chunks(
        me, selected, query,
        [((near,), lambda m, s, h: wants(s, m ^ 1, h, per_owner), stacked),
         ((mid_keys, mid_values), lambda m, s, h: inner(m) & wants(s, m ^ 3, h, per_owner), middle),
         ((far,), lambda m, s, h: outer(m) & wants(s, m ^ 3, h, per_owner), stacked)],
        state, group, kv_heads, 1)
    out = None
    for h in heads:
        out = finish(me, selected, query, (cross[h],), lambda m, s, h: wants(s, m ^ 2, h, per_owner),
                     single, state, group, h, out)
    return out


def solution(mesh):
    kv = P(("groups", "ctx"), "mp")
    plan = line_of_four if mesh.shape["ctx"] == 4 else gathered

    def per_device(query, span_keys, span_values, cache_keys, stored_values, selected):
        group = query.shape[1] // span_keys.shape[1]
        return plan(query, span_keys, span_values, cache_keys, stored_values, selected, group)

    return jax.shard_map(
        per_device, mesh=mesh, in_specs=(kv, kv, kv, kv, kv, P(("groups", "ctx"), "mp", None)),
        out_specs=kv, check_vma=False)
```

```python
import jax
import jax.numpy as jnp
from jax import lax
from jax.experimental import pallas as pl
from jax.experimental.pallas import tpu as pltpu
from jax.sharding import PartitionSpec as P

HEAD = 128
LOG2E = 1.4426950408889634
NEG = -1e30
VMEM = pl.BlockSpec(memory_space=pltpu.VMEM)
ANY = pl.BlockSpec(memory_space=pl.ANY)
SMEM = pl.BlockSpec(memory_space=pltpu.SMEM)
PARAMS = pltpu.CompilerParams(vmem_limit_bytes=8 << 20)
WIDE = pltpu.CompilerParams(vmem_limit_bytes=20 << 20)


def near_core(x):
    return pltpu.with_memory_space_constraint(x, pltpu.VMEM)


def in_hbm(x):
    return pltpu.with_memory_space_constraint(x, pltpu.HBM)


def local_row(sel, owner, h, per_owner, at=0):
    a, b = sel[at, h, 0], sel[at, h, 1]
    lo = owner * per_owner
    in_a = (a >= lo) & (a < lo + per_owner)
    in_b = (b >= lo) & (b < lo + per_owner)
    return jnp.where(in_a, a - lo, jnp.where(in_b, b - lo, 0))


def wants(sel, owner, h, per_owner):
    a, b = sel[0, h, 0], sel[0, h, 1]
    lo = owner * per_owner
    return ((a >= lo) & (a < lo + per_owner)) | ((b >= lo) & (b < lo + per_owner))


def with_ones(v):
    return jnp.concatenate([v, jnp.ones((v.shape[0], HEAD), jnp.bfloat16)], axis=1)


def scores_of(q, k):
    return lax.dot_general(q, k, (((1,), (1,)), ((), ())), preferred_element_type=jnp.float32)


SCALE = LOG2E * HEAD ** -0.5


def own_rest(s, v, mask, first_key):
    s = jnp.concatenate([s[:, :first_key], s[:, first_key:] + mask], axis=1) if first_key else s + mask
    top = jnp.max(s, axis=1, keepdims=True)
    p = jnp.exp2((s - top) * SCALE).astype(jnp.bfloat16)
    sums = jnp.dot(p, v, preferred_element_type=jnp.float32)
    return sums[:, :HEAD], sums[:, HEAD:], jnp.broadcast_to(top, (s.shape[0], HEAD))


def chunk_tile(q, k, v, acc, den, old):
    s = scores_of(q, k)
    top = jnp.maximum(old, jnp.max(s, axis=1, keepdims=True))
    p = jnp.concatenate(
        [jnp.exp2((s[:, j:j + HEAD] - top) * SCALE) for j in range(0, s.shape[1], HEAD)], axis=1).astype(jnp.bfloat16)
    sums = jnp.dot(p, v, preferred_element_type=jnp.float32)
    keep = jnp.exp2((old - top) * SCALE)
    return acc * keep + sums[:, :HEAD], den * keep + sums[:, HEAD:], top


def cell(r, tile, head):
    rows = slice(r * tile, (r + 1) * tile)
    if isinstance(head, int):
        return rows, slice(head * HEAD, (head + 1) * HEAD)
    return rows, pl.ds(pl.multiple_of(head * HEAD, HEAD), HEAD)


def column(h, width=HEAD):
    return slice(h * width, (h + 1) * width) if isinstance(h, int) else pl.ds(pl.multiple_of(h * width, width), width)


def state_shapes(query):
    return [pltpu.VMEM(query.shape, jnp.float32)] * 3


def cost(rows, heads, blocks):
    work = rows * rows * heads * blocks
    return pl.CostEstimate(flops=4 * work * HEAD, transcendentals=work, bytes_accessed=rows * heads * HEAD * 16)


def add_chunk(q_ref, before, state, kv, h, group, tile):
    k, v = kv
    v = with_ones(v)
    for i in range(group):
        for r in range(q_ref.shape[0] // tile):
            at = cell(r, tile, h * group + i)
            new = chunk_tile(q_ref[at], k, v, before[0][at], before[1][at], before[2][at])
            for ref, value in zip(state, new):
                ref[at] = value


def own_and_local(me, sel, query, span_keys, span_values, keys, values, per_owner, group):
    rows, half = query.shape[0], query.shape[0] // 2
    kv_heads = span_keys.shape[1] // HEAD

    def body(me_ref, sel_ref, q_ref, sk_ref, sv_ref, k_ref, v_ref, *refs):
        state, mask_ref = refs[:3], refs[3]
        qpos = lax.broadcasted_iota(jnp.int32, (half, half), 0)
        kpos = lax.broadcasted_iota(jnp.int32, (half, half), 1)
        mask_ref[...] = jnp.where(kpos <= qpos, 0.0, NEG)

        def one_head(h, carry):
            col = column(h)
            own_k, own_v = sk_ref[:, col], with_ones(sv_ref[:, col])
            work = [(r, cell(r, half, h * group + i)) for r in range(2) for i in range(group)]
            queries = [q_ref[at] for _, at in work]

            def scores(j):
                return scores_of(queries[j], own_k[:(work[j][0] + 1) * half])

            done, s = [], scores(0)
            for j, (r, at) in enumerate(work):
                following = scores(j + 1) if j + 1 < len(work) else None
                done.append(own_rest(s, own_v[:(r + 1) * half], mask_ref[...], r * half))
                s = following
            for (_, at), new in zip(work, done):
                for ref, value in zip(state, new):
                    ref[at] = value
            if per_owner:
                @pl.when(wants(sel_ref, me_ref[0], h, per_owner))
                def _():
                    at = pl.ds(pl.multiple_of(local_row(sel_ref, me_ref[0], h, per_owner) * rows, rows), rows)
                    add_chunk(q_ref, state, state, (k_ref[at, col], v_ref[at, col]), h, group, rows // 4)
            return carry

        lax.fori_loop(0, kv_heads, one_head, 0)

    return pl.pallas_call(
        body, out_shape=state_shapes(query), in_specs=[SMEM] * 2 + [VMEM] * 5, out_specs=[VMEM] * 3,
        scratch_shapes=[pltpu.VMEM((half, half), jnp.float32)],
        compiler_params=WIDE, cost_estimate=cost(rows, kv_heads * group, 2),
    )(me, sel, *map(in_hbm, (query, span_keys, span_values, keys, values)))


def more_chunks(me, sel, query, sources, state, group, kv_heads, blocks):
    rows, half = query.shape[0], query.shape[0] // 2
    arrays = [a for s in sources for a in s[0]]

    def body(me_ref, sel_ref, q_ref, *refs):
        refs, old, state = refs[:len(arrays)], refs[len(arrays):len(arrays) + 3], refs[len(arrays) + 3:]
        def one_head(h, carry):
            cols = column(h, group * HEAD)
            at = 0
            for i, source in enumerate(sources):
                mine = refs[at:at + len(source[0])]
                at += len(source[0])
                needed = source[1](me_ref[0], sel_ref, h)

                @pl.when(needed)
                def _():
                    kv = source[2](mine, me_ref[0], sel_ref, h)
                    add_chunk(q_ref, state if i else old, state, kv, h, group, rows // 4)

                if i == 0:
                    @pl.when(jnp.logical_not(needed))
                    def _():
                        for new, previous in zip(state, old):
                            new[:, cols] = previous[:, cols]
            return carry

        lax.fori_loop(0, kv_heads, one_head, 0)

    n = 3 + len(arrays)
    return pl.pallas_call(
        body, out_shape=state_shapes(query), in_specs=[SMEM] * 2 + [VMEM] * (n + 1), out_specs=[VMEM] * 3,
        compiler_params=PARAMS, cost_estimate=cost(rows, kv_heads * group, blocks),
    )(me, sel, *map(near_core, (query, *arrays, *state)))


def finish(me, sel, query, arrays, when, read, state, group, head, out):
    rows = query.shape[0]
    tile = rows // 4
    first = head * group

    def body(me_ref, sel_ref, q_ref, *refs):
        refs, state, (o_ref, buf, sem) = refs[:len(arrays)], refs[len(arrays):len(arrays) + 3], refs[-3:]

        def tiles(fn):
            copies = []
            for i in range(group):
                for r in range(rows // tile):
                    acc, den = fn(cell(r, tile, first + i))
                    buf[cell(r, tile, i)] = (acc / den).astype(jnp.bfloat16)
                copies.append(pltpu.make_async_copy(
                    buf.at[:, pl.ds(i * HEAD, HEAD)], o_ref.at[:, pl.ds((first + i) * HEAD, HEAD)], sem.at[i]))
                copies[-1].start()
            for copy in copies:
                copy.wait()

        needed = when(me_ref[0], sel_ref, head)

        @pl.when(needed)
        def _():
            k, v = read(refs, me_ref[0], sel_ref, head)
            v = with_ones(v)
            tiles(lambda at: chunk_tile(q_ref[at], k, v, state[0][at], state[1][at], state[2][at])[:2])

        @pl.when(jnp.logical_not(needed))
        def _():
            tiles(lambda at: (state[0][at], state[1][at]))

    extra = [] if out is None else [out]
    n = 6 + len(arrays)
    return pl.pallas_call(
        body, out_shape=jax.ShapeDtypeStruct(query.shape, jnp.bfloat16),
        in_specs=[SMEM] * 2 + [VMEM] * (n - 2) + [ANY] * len(extra), out_specs=ANY,
        scratch_shapes=[pltpu.VMEM((rows, group * HEAD), jnp.bfloat16), pltpu.SemaphoreType.DMA((group,))],
        input_output_aliases={n: 0} if extra else {},
        compiler_params=PARAMS, cost_estimate=cost(rows, group, 1),
    )(me, sel, *map(near_core, (query, *arrays, *state)), *extra)


def pick(me, sels, arrays, rows, jobs, place=near_core):
    n, k = len(sels), len(arrays)

    def body(me_ref, *refs):
        sel_refs, refs, outs = refs[:n], refs[n:n + k], refs[n + k:]
        for out, parts in zip(outs, jobs):
            for when, keys, values, row, h, slot in parts:
                def copy():
                    at = pl.ds(pl.multiple_of(row(me_ref[0], sel_refs, h) * rows, rows), rows)
                    col = slice(h * HEAD, (h + 1) * HEAD)
                    out[2 * slot * rows:(2 * slot + 1) * rows] = refs[keys][at, col]
                    out[(2 * slot + 1) * rows:(2 * slot + 2) * rows] = refs[values][at, col]
                if when is None:
                    copy()
                else:
                    pl.when(when(me_ref[0]))(copy)

    shapes = [pltpu.VMEM((2 * rows * (1 + max(p[5] for p in parts)), HEAD), jnp.bfloat16) for parts in jobs]
    return pl.pallas_call(
        body, out_shape=shapes, in_specs=[SMEM] * (1 + n) + [VMEM] * k, out_specs=[VMEM] * len(jobs),
        compiler_params=PARAMS,
        cost_estimate=pl.CostEstimate(flops=0, transcendentals=0, bytes_accessed=8 * rows * HEAD * len(jobs)),
    )(me, *sels, *map(place, arrays))


def gathered(query, span_keys, span_values, cache_keys, stored_values, selected, group):
    rows = query.shape[0]
    kv_heads = span_keys.shape[1] // HEAD
    me = lax.axis_index("ctx").astype(jnp.int32).reshape(1)
    keys = lax.all_gather(cache_keys, "ctx", axis=0, tiled=True)
    values = lax.all_gather(stored_values, "ctx", axis=0, tiled=True)
    state = own_and_local(me, selected, query, span_keys, span_values, cache_keys, stored_values, 0, group)

    def always(m, s, h):
        return m >= 0

    def chosen(array, h, slot):
        start = jnp.clip(selected[0, h, slot], 0, keys.shape[0] // rows - 1) * rows
        return lax.dynamic_slice(array, (start, h * HEAD), (rows, HEAD))

    def stacked(refs, m, s, h):
        start = pl.multiple_of(2 * h * rows, rows)
        return refs[0][pl.ds(start, rows)], refs[0][pl.ds(start + rows, rows)]

    blocks = [[jnp.concatenate([chosen(a, h, slot) for h in range(kv_heads) for a in (keys, values)])] for slot in range(2)]
    state = more_chunks(me, selected, query, [(blocks[0], always, stacked)], state, group, kv_heads, 1)
    out = None
    for h in range(kv_heads):
        out = finish(me, selected, query, blocks[1], always, stacked, state, group, h, out)
    return out


def line_of_four(query, span_keys, span_values, cache_keys, stored_values, selected, group):
    rows = query.shape[0]
    kv_heads = span_keys.shape[1] // HEAD
    per_owner = cache_keys.shape[0] // rows
    me = lax.axis_index("ctx").astype(jnp.int32).reshape(1)
    heads = range(kv_heads)

    def inner(m):
        return (m == 1) | (m == 2)

    def outer(m):
        return (m == 0) | (m == 3)

    sel1 = lax.ppermute(selected, "ctx", [(0, 1), (1, 0), (2, 3), (3, 2)])
    mid_keys = lax.ppermute(cache_keys, "ctx", [(1, 2), (2, 1)])
    mid_values = lax.ppermute(stored_values, "ctx", [(1, 2), (2, 1)])
    both = lax.ppermute(jnp.concatenate([selected, sel1], axis=0), "ctx", [(3, 0), (0, 3)])

    *near_out, far_out = pick(
        me, (sel1, both), (cache_keys, stored_values), rows,
        [[(None, 0, 1, lambda m, s, h: local_row(s[0], m, h, per_owner), h, 0)] for h in heads] +
        [[(outer, 0, 1, lambda m, s, h: local_row(s[1], m, h, per_owner), h, h) for h in heads]], in_hbm)
    near = [lax.ppermute(n, "ctx", [(0, 1), (1, 0), (2, 3), (3, 2)]) for n in near_out]
    far = lax.ppermute(far_out, "ctx", [(0, 3), (3, 0)])

    near_out, far_out, span_keys = lax.optimization_barrier((near_out, far_out, span_keys))
    state = own_and_local(me, selected, query, span_keys, span_values, cache_keys, stored_values, per_owner, group)

    def single(refs, m, s, h):
        return refs[0][:rows], refs[0][rows:]

    near, state = lax.optimization_barrier((near, state))
    state = more_chunks(
        me, selected, query,
        [((near[i],), lambda m, s, h, i=i: (h == i) & wants(s, m ^ 1, h, per_owner), single) for i in heads],
        state, group, kv_heads, 1)

    mid_keys, mid_values, state = lax.optimization_barrier((mid_keys, mid_values, state))
    cross_out = pick(
        me, (sel1, both), (cache_keys, stored_values, mid_keys, mid_values), rows,
        [[(inner, 2, 3, lambda m, s, h: local_row(s[0], m ^ 3, h, per_owner), h, 0),
          (outer, 0, 1, lambda m, s, h: local_row(s[1], m, h, per_owner, 1), h, 0)] for h in heads])
    cross = [lax.ppermute(c, "ctx", [(0, 2), (3, 1), (1, 0), (2, 3)]) for c in cross_out]

    def stacked(refs, m, s, h):
        start = pl.multiple_of(2 * h * rows, rows)
        return refs[0][pl.ds(start, rows)], refs[0][pl.ds(start + rows, rows)]

    def middle(refs, m, s, h):
        at = pl.ds(pl.multiple_of(local_row(s, m ^ 3, h, per_owner) * rows, rows), rows)
        return refs[0][at, column(h)], refs[1][at, column(h)]

    far, cross_out, state = lax.optimization_barrier((far, cross_out, state))
    state = more_chunks(
        me, selected, query,
        [((mid_keys, mid_values), lambda m, s, h: inner(m) & wants(s, m ^ 3, h, per_owner), middle),
         ((far,), lambda m, s, h: outer(m) & wants(s, m ^ 3, h, per_owner), stacked)],
        state, group, kv_heads, 1)
    out = None
    for h in heads:
        out = finish(me, selected, query, (cross[h],), lambda m, s, h: wants(s, m ^ 2, h, per_owner),
                     single, state, group, h, out)
    return out


def solution(mesh):
    kv = P(("groups", "ctx"), "mp")
    plan = line_of_four if mesh.shape["ctx"] == 4 else gathered

    def per_device(query, span_keys, span_values, cache_keys, stored_values, selected):
        group = query.shape[1] // span_keys.shape[1]
        return plan(query, span_keys, span_values, cache_keys, stored_values, selected, group)

    return jax.shard_map(
        per_device, mesh=mesh, in_specs=(kv, kv, kv, kv, kv, P(("groups", "ctx"), "mp", None)),
        out_specs=kv, check_vma=False)
```

```python
import jax
import jax.numpy as jnp
from jax import lax
from jax.experimental import pallas as pl
from jax.experimental.pallas import tpu as pltpu
from jax.sharding import PartitionSpec as P

HEAD = 128
LOG2E = 1.4426950408889634
NEG = -1e30
VMEM = pl.BlockSpec(memory_space=pltpu.VMEM)
ANY = pl.BlockSpec(memory_space=pl.ANY)
SMEM = pl.BlockSpec(memory_space=pltpu.SMEM)
PARAMS = pltpu.CompilerParams(vmem_limit_bytes=8 << 20)
WIDE = pltpu.CompilerParams(vmem_limit_bytes=20 << 20)


def near_core(x):
    return pltpu.with_memory_space_constraint(x, pltpu.VMEM)


def in_hbm(x):
    return pltpu.with_memory_space_constraint(x, pltpu.HBM)


def local_row(sel, owner, h, per_owner, at=0):
    a, b = sel[at, h, 0], sel[at, h, 1]
    lo = owner * per_owner
    in_a = (a >= lo) & (a < lo + per_owner)
    in_b = (b >= lo) & (b < lo + per_owner)
    return jnp.where(in_a, a - lo, jnp.where(in_b, b - lo, 0))


def wants(sel, owner, h, per_owner):
    a, b = sel[0, h, 0], sel[0, h, 1]
    lo = owner * per_owner
    return ((a >= lo) & (a < lo + per_owner)) | ((b >= lo) & (b < lo + per_owner))


def with_ones(v):
    return jnp.concatenate([v, jnp.ones((v.shape[0], HEAD), jnp.bfloat16)], axis=1)


def scores_of(q, k):
    return lax.dot_general(q, k, (((1,), (1,)), ((), ())), preferred_element_type=jnp.float32)


SCALE = LOG2E * HEAD ** -0.5


def own_rest(s, v, mask, first_key):
    s = jnp.concatenate([s[:, :first_key], s[:, first_key:] + mask], axis=1) if first_key else s + mask
    top = jnp.max(s, axis=1, keepdims=True)
    p = jnp.exp2((s - top) * SCALE).astype(jnp.bfloat16)
    sums = jnp.dot(p, v, preferred_element_type=jnp.float32)
    return sums[:, :HEAD], sums[:, HEAD:], jnp.broadcast_to(top, (s.shape[0], HEAD))


def chunk_tile(q, k, v, acc, den, old):
    s = scores_of(q, k)
    top = jnp.maximum(old, jnp.max(s, axis=1, keepdims=True))
    p = jnp.concatenate(
        [jnp.exp2((s[:, j:j + HEAD] - top) * SCALE) for j in range(0, s.shape[1], HEAD)], axis=1).astype(jnp.bfloat16)
    sums = jnp.dot(p, v, preferred_element_type=jnp.float32)
    keep = jnp.exp2((old - top) * SCALE)
    return acc * keep + sums[:, :HEAD], den * keep + sums[:, HEAD:], top


def cell(r, tile, head):
    rows = slice(r * tile, (r + 1) * tile)
    if isinstance(head, int):
        return rows, slice(head * HEAD, (head + 1) * HEAD)
    return rows, pl.ds(pl.multiple_of(head * HEAD, HEAD), HEAD)


def column(h, width=HEAD):
    return slice(h * width, (h + 1) * width) if isinstance(h, int) else pl.ds(pl.multiple_of(h * width, width), width)


def state_shapes(query):
    return [pltpu.VMEM(query.shape, jnp.float32)] * 3


def cost(rows, heads, blocks):
    work = rows * rows * heads * blocks
    return pl.CostEstimate(flops=4 * work * HEAD, transcendentals=work, bytes_accessed=rows * heads * HEAD * 16)


def add_chunk(q_ref, before, state, kv, h, group, tile):
    k, v = kv
    v = with_ones(v)
    for i in range(group):
        for r in range(q_ref.shape[0] // tile):
            at = cell(r, tile, h * group + i)
            new = chunk_tile(q_ref[at], k, v, before[0][at], before[1][at], before[2][at])
            for ref, value in zip(state, new):
                ref[at] = value


def own_and_local(me, sel, query, span_keys, span_values, keys, values, per_owner, group):
    rows, half = query.shape[0], query.shape[0] // 2
    kv_heads = span_keys.shape[1] // HEAD

    def body(me_ref, sel_ref, q_ref, sk_ref, sv_ref, k_ref, v_ref, *refs):
        state, mask_ref = refs[:3], refs[3]
        qpos = lax.broadcasted_iota(jnp.int32, (half, half), 0)
        kpos = lax.broadcasted_iota(jnp.int32, (half, half), 1)
        mask_ref[...] = jnp.where(kpos <= qpos, 0.0, NEG)

        def one_head(h, carry):
            col = column(h)
            own_k, own_v = sk_ref[:, col], with_ones(sv_ref[:, col])
            work = [(r, cell(r, half, h * group + i)) for r in range(2) for i in range(group)]
            queries = [q_ref[at] for _, at in work]

            def scores(j):
                return scores_of(queries[j], own_k[:(work[j][0] + 1) * half])

            done, s = [], scores(0)
            for j, (r, at) in enumerate(work):
                following = scores(j + 1) if j + 1 < len(work) else None
                done.append(own_rest(s, own_v[:(r + 1) * half], mask_ref[...], r * half))
                s = following
            for (_, at), new in zip(work, done):
                for ref, value in zip(state, new):
                    ref[at] = value
            if per_owner:
                @pl.when(wants(sel_ref, me_ref[0], h, per_owner))
                def _():
                    at = pl.ds(pl.multiple_of(local_row(sel_ref, me_ref[0], h, per_owner) * rows, rows), rows)
                    add_chunk(q_ref, state, state, (k_ref[at, col], v_ref[at, col]), h, group, rows // 4)
            return carry

        lax.fori_loop(0, kv_heads, one_head, 0)

    return pl.pallas_call(
        body, out_shape=state_shapes(query), in_specs=[SMEM] * 2 + [VMEM] * 5, out_specs=[VMEM] * 3,
        scratch_shapes=[pltpu.VMEM((half, half), jnp.float32)],
        compiler_params=WIDE, cost_estimate=cost(rows, kv_heads * group, 2),
    )(me, sel, *map(in_hbm, (query, span_keys, span_values, keys, values)))


def more_chunks(me, sel, query, sources, state, group, kv_heads, blocks):
    rows, half = query.shape[0], query.shape[0] // 2
    arrays = [a for s in sources for a in s[0]]

    def body(me_ref, sel_ref, q_ref, *refs):
        refs, old, state = refs[:len(arrays)], refs[len(arrays):len(arrays) + 3], refs[len(arrays) + 3:]
        def one_head(h, carry):
            cols = column(h, group * HEAD)
            at = 0
            for i, source in enumerate(sources):
                mine = refs[at:at + len(source[0])]
                at += len(source[0])
                needed = source[1](me_ref[0], sel_ref, h)

                @pl.when(needed)
                def _():
                    kv = source[2](mine, me_ref[0], sel_ref, h)
                    add_chunk(q_ref, state if i else old, state, kv, h, group, rows // 4)

                if i == 0:
                    @pl.when(jnp.logical_not(needed))
                    def _():
                        for new, previous in zip(state, old):
                            new[:, cols] = previous[:, cols]
            return carry

        lax.fori_loop(0, kv_heads, one_head, 0)

    n = 3 + len(arrays)
    return pl.pallas_call(
        body, out_shape=state_shapes(query), in_specs=[SMEM] * 2 + [VMEM] * (n + 1), out_specs=[VMEM] * 3,
        compiler_params=PARAMS, cost_estimate=cost(rows, kv_heads * group, blocks),
    )(me, sel, *map(near_core, (query, *arrays, *state)))


def finish(me, sel, query, arrays, when, read, state, group, head, out):
    rows = query.shape[0]
    tile = rows // 4
    first = head * group

    def body(me_ref, sel_ref, q_ref, *refs):
        refs, state, (o_ref, buf, sem) = refs[:len(arrays)], refs[len(arrays):len(arrays) + 3], refs[-3:]

        def tiles(fn):
            copies = []
            for i in range(group):
                for r in range(rows // tile):
                    acc, den = fn(cell(r, tile, first + i))
                    buf[cell(r, tile, i)] = (acc / den).astype(jnp.bfloat16)
                copies.append(pltpu.make_async_copy(
                    buf.at[:, pl.ds(i * HEAD, HEAD)], o_ref.at[:, pl.ds((first + i) * HEAD, HEAD)], sem.at[i]))
                copies[-1].start()
            for copy in copies:
                copy.wait()

        needed = when(me_ref[0], sel_ref, head)

        @pl.when(needed)
        def _():
            k, v = read(refs, me_ref[0], sel_ref, head)
            v = with_ones(v)
            tiles(lambda at: chunk_tile(q_ref[at], k, v, state[0][at], state[1][at], state[2][at])[:2])

        @pl.when(jnp.logical_not(needed))
        def _():
            tiles(lambda at: (state[0][at], state[1][at]))

    extra = [] if out is None else [out]
    n = 6 + len(arrays)
    return pl.pallas_call(
        body, out_shape=jax.ShapeDtypeStruct(query.shape, jnp.bfloat16),
        in_specs=[SMEM] * 2 + [VMEM] * (n - 2) + [ANY] * len(extra), out_specs=ANY,
        scratch_shapes=[pltpu.VMEM((rows, group * HEAD), jnp.bfloat16), pltpu.SemaphoreType.DMA((group,))],
        input_output_aliases={n: 0} if extra else {},
        compiler_params=PARAMS, cost_estimate=cost(rows, group, 1),
    )(me, sel, *map(near_core, (query, *arrays, *state)), *extra)


def pick(me, sels, arrays, rows, jobs, place=near_core):
    n, k = len(sels), len(arrays)

    def body(me_ref, *refs):
        sel_refs, refs, outs = refs[:n], refs[n:n + k], refs[n + k:]
        for out, parts in zip(outs, jobs):
            for when, keys, values, row, h, slot in parts:
                def copy():
                    at = pl.ds(pl.multiple_of(row(me_ref[0], sel_refs, h) * rows, rows), rows)
                    col = slice(h * HEAD, (h + 1) * HEAD)
                    out[2 * slot * rows:(2 * slot + 1) * rows] = refs[keys][at, col]
                    out[(2 * slot + 1) * rows:(2 * slot + 2) * rows] = refs[values][at, col]
                if when is None:
                    copy()
                else:
                    pl.when(when(me_ref[0]))(copy)

    shapes = [pltpu.VMEM((2 * rows * (1 + max(p[5] for p in parts)), HEAD), jnp.bfloat16) for parts in jobs]
    return pl.pallas_call(
        body, out_shape=shapes, in_specs=[SMEM] * (1 + n) + [VMEM] * k, out_specs=[VMEM] * len(jobs),
        compiler_params=PARAMS,
        cost_estimate=pl.CostEstimate(flops=0, transcendentals=0, bytes_accessed=8 * rows * HEAD * len(jobs)),
    )(me, *sels, *map(place, arrays))


def gathered(query, span_keys, span_values, cache_keys, stored_values, selected, group):
    rows = query.shape[0]
    kv_heads = span_keys.shape[1] // HEAD
    me = lax.axis_index("ctx").astype(jnp.int32).reshape(1)
    keys = lax.all_gather(cache_keys, "ctx", axis=0, tiled=True)
    values = lax.all_gather(stored_values, "ctx", axis=0, tiled=True)
    state = own_and_local(me, selected, query, span_keys, span_values, cache_keys, stored_values, 0, group)

    def always(m, s, h):
        return m >= 0

    def chosen(array, h, slot):
        start = jnp.clip(selected[0, h, slot], 0, keys.shape[0] // rows - 1) * rows
        return lax.dynamic_slice(array, (start, h * HEAD), (rows, HEAD))

    def stacked(refs, m, s, h):
        start = pl.multiple_of(2 * h * rows, rows)
        return refs[0][pl.ds(start, rows)], refs[0][pl.ds(start + rows, rows)]

    blocks = [[jnp.concatenate([chosen(a, h, slot) for h in range(kv_heads) for a in (keys, values)])] for slot in range(2)]
    state = more_chunks(me, selected, query, [(blocks[0], always, stacked)], state, group, kv_heads, 1)
    out = None
    for h in range(kv_heads):
        out = finish(me, selected, query, blocks[1], always, stacked, state, group, h, out)
    return out


def line_of_four(query, span_keys, span_values, cache_keys, stored_values, selected, group):
    rows = query.shape[0]
    kv_heads = span_keys.shape[1] // HEAD
    per_owner = cache_keys.shape[0] // rows
    me = lax.axis_index("ctx").astype(jnp.int32).reshape(1)
    heads = range(kv_heads)

    def inner(m):
        return (m == 1) | (m == 2)

    def outer(m):
        return (m == 0) | (m == 3)

    sel1 = lax.ppermute(selected, "ctx", [(0, 1), (1, 0), (2, 3), (3, 2)])
    mid_keys = lax.ppermute(cache_keys, "ctx", [(1, 2), (2, 1)])
    mid_values = lax.ppermute(stored_values, "ctx", [(1, 2), (2, 1)])
    both = lax.ppermute(jnp.concatenate([selected, sel1], axis=0), "ctx", [(3, 0), (0, 3)])

    out = pick(
        me, (sel1, both), (cache_keys, stored_values), rows,
        [[(None, 0, 1, lambda m, s, h: local_row(s[0], m, h, per_owner), h, 0)] for h in heads] +
        [[(outer, 0, 1, lambda m, s, h: local_row(s[1], m, h, per_owner), h, 0)] for h in heads], in_hbm)
    near_out, far_out = out[:kv_heads], out[kv_heads:]
    near = [lax.ppermute(n, "ctx", [(0, 1), (1, 0), (2, 3), (3, 2)]) for n in near_out]
    far = [lax.ppermute(f, "ctx", [(0, 3), (3, 0)]) for f in far_out[:-1]]

    near_out, far_out, span_keys = lax.optimization_barrier((near_out, far_out, span_keys))
    state = own_and_local(me, selected, query, span_keys, span_values, cache_keys, stored_values, per_owner, group)
    far_last, state = lax.optimization_barrier((far_out[-1], state))
    last = lax.ppermute(far_last, "ctx", [(0, 3), (3, 0)])
    far_last, state = lax.optimization_barrier((far_last, state))

    def single(refs, m, s, h):
        return refs[0][:rows], refs[0][rows:]

    near, far, state = lax.optimization_barrier((near, far, state))

    def stack(refs, m, s, h):
        k, v = refs[0][:rows], refs[0][rows:]
        for i in range(1, len(refs)):
            k, v = jnp.where(h == i, refs[i][:rows], k), jnp.where(h == i, refs[i][rows:], v)
        return k, v

    state = more_chunks(
        me, selected, query,
        [(tuple(near), lambda m, s, h: wants(s, m ^ 1, h, per_owner) & jnp.logical_not(wants(s, m, h, per_owner)), stack),
         (tuple(far), lambda m, s, h: outer(m) & (h < kv_heads - 1) & wants(s, m ^ 3, h, per_owner)
          & wants(s, m ^ 2, h, per_owner), stack)],
        state, group, kv_heads, 1)

    mid_keys, mid_values, state = lax.optimization_barrier((mid_keys, mid_values, state))
    cross_out = pick(
        me, (sel1, both), (cache_keys, stored_values, mid_keys, mid_values), rows,
        [[(inner, 2, 3, lambda m, s, h: local_row(s[0], m ^ 3, h, per_owner), h, 0),
          (outer, 0, 1, lambda m, s, h: local_row(s[1], m, h, per_owner, 1), h, 0)] for h in heads])
    cross = [lax.ppermute(c, "ctx", [(0, 2), (3, 1), (1, 0), (2, 3)]) for c in cross_out]

    def stacked(refs, m, s, h):
        start = pl.multiple_of(2 * h * rows, rows)
        return refs[0][pl.ds(start, rows)], refs[0][pl.ds(start + rows, rows)]

    def middle(refs, m, s, h):
        at = pl.ds(pl.multiple_of(local_row(s, m ^ 3, h, per_owner) * rows, rows), rows)
        return refs[0][at, column(h)], refs[1][at, column(h)]

    last, cross_out, state = lax.optimization_barrier((last, cross_out, state))
    state = more_chunks(
        me, selected, query,
        [((mid_keys, mid_values), lambda m, s, h: inner(m) & wants(s, m ^ 3, h, per_owner), middle),
         ((*far, last), lambda m, s, h: outer(m) & wants(s, m ^ 3, h, per_owner)
          & ((h == kv_heads - 1) | jnp.logical_not(wants(s, m ^ 2, h, per_owner))), stack),
         (tuple(near), lambda m, s, h: wants(s, m ^ 1, h, per_owner) & wants(s, m, h, per_owner), stack)],
        state, group, kv_heads, 1)
    out = None
    for h in heads:
        out = finish(me, selected, query, (cross[h],), lambda m, s, h: wants(s, m ^ 2, h, per_owner),
                     single, state, group, h, out)
    return out


def solution(mesh):
    kv = P(("groups", "ctx"), "mp")
    plan = line_of_four if mesh.shape["ctx"] == 4 else gathered

    def per_device(query, span_keys, span_values, cache_keys, stored_values, selected):
        group = query.shape[1] // span_keys.shape[1]
        return plan(query, span_keys, span_values, cache_keys, stored_values, selected, group)

    return jax.shard_map(
        per_device, mesh=mesh, in_specs=(kv, kv, kv, kv, kv, P(("groups", "ctx"), "mp", None)),
        out_specs=kv, check_vma=False)
```

```python
import jax
import jax.numpy as jnp
from jax import lax
from jax.experimental import pallas as pl
from jax.experimental.pallas import tpu as pltpu
from jax.sharding import PartitionSpec as P

HEAD = 128
LOG2E = 1.4426950408889634
NEG = -1e30
VMEM = pl.BlockSpec(memory_space=pltpu.VMEM)
ANY = pl.BlockSpec(memory_space=pl.ANY)
SMEM = pl.BlockSpec(memory_space=pltpu.SMEM)
PARAMS = pltpu.CompilerParams(vmem_limit_bytes=8 << 20)
WIDE = pltpu.CompilerParams(vmem_limit_bytes=20 << 20)


def near_core(x):
    return pltpu.with_memory_space_constraint(x, pltpu.VMEM)


def in_hbm(x):
    return pltpu.with_memory_space_constraint(x, pltpu.HBM)


def local_row(sel, owner, h, per_owner, at=0):
    a, b = sel[at, h, 0], sel[at, h, 1]
    lo = owner * per_owner
    in_a = (a >= lo) & (a < lo + per_owner)
    in_b = (b >= lo) & (b < lo + per_owner)
    return jnp.where(in_a, a - lo, jnp.where(in_b, b - lo, 0))


def wants(sel, owner, h, per_owner):
    a, b = sel[0, h, 0], sel[0, h, 1]
    lo = owner * per_owner
    return ((a >= lo) & (a < lo + per_owner)) | ((b >= lo) & (b < lo + per_owner))


def with_ones(v):
    return jnp.concatenate([v, jnp.ones((v.shape[0], HEAD), jnp.bfloat16)], axis=1)


def scores_of(q, k):
    return lax.dot_general(q, k, (((1,), (1,)), ((), ())), preferred_element_type=jnp.float32)


SCALE = LOG2E * HEAD ** -0.5


def own_rest(s, v, mask, first_key):
    s = jnp.concatenate([s[:, :first_key], s[:, first_key:] + mask], axis=1) if first_key else s + mask
    top = jnp.max(s, axis=1, keepdims=True)
    p = jnp.exp2((s - top) * SCALE).astype(jnp.bfloat16)
    sums = jnp.dot(p, v, preferred_element_type=jnp.float32)
    return sums[:, :HEAD], sums[:, HEAD:], jnp.broadcast_to(top, (s.shape[0], HEAD))


def chunk_tile(q, k, v, acc, den, old):
    s = scores_of(q, k)
    top = jnp.maximum(old, jnp.max(s, axis=1, keepdims=True))
    p = jnp.concatenate(
        [jnp.exp2((s[:, j:j + HEAD] - top) * SCALE) for j in range(0, s.shape[1], HEAD)], axis=1).astype(jnp.bfloat16)
    sums = jnp.dot(p, v, preferred_element_type=jnp.float32)
    keep = jnp.exp2((old - top) * SCALE)
    return acc * keep + sums[:, :HEAD], den * keep + sums[:, HEAD:], top


def cell(r, tile, head):
    rows = slice(r * tile, (r + 1) * tile)
    if isinstance(head, int):
        return rows, slice(head * HEAD, (head + 1) * HEAD)
    return rows, pl.ds(pl.multiple_of(head * HEAD, HEAD), HEAD)


def column(h, width=HEAD):
    return slice(h * width, (h + 1) * width) if isinstance(h, int) else pl.ds(pl.multiple_of(h * width, width), width)


def state_shapes(query):
    return [pltpu.VMEM(query.shape, jnp.float32)] * 3


def cost(rows, heads, blocks):
    work = rows * rows * heads * blocks
    return pl.CostEstimate(flops=4 * work * HEAD, transcendentals=work, bytes_accessed=rows * heads * HEAD * 16)


def add_chunk(q_ref, before, state, kv, h, group, tile):
    k, v = kv
    v = with_ones(v)
    for i in range(group):
        for r in range(q_ref.shape[0] // tile):
            at = cell(r, tile, h * group + i)
            new = chunk_tile(q_ref[at], k, v, before[0][at], before[1][at], before[2][at])
            for ref, value in zip(state, new):
                ref[at] = value


def own_and_local(me, sel, query, span_keys, span_values, keys, values, per_owner, group):
    rows, half = query.shape[0], query.shape[0] // 2
    kv_heads = span_keys.shape[1] // HEAD

    def body(me_ref, sel_ref, q_ref, sk_ref, sv_ref, k_ref, v_ref, *refs):
        state, mask_ref = refs[:3], refs[3]
        qpos = lax.broadcasted_iota(jnp.int32, (half, half), 0)
        kpos = lax.broadcasted_iota(jnp.int32, (half, half), 1)
        mask_ref[...] = jnp.where(kpos <= qpos, 0.0, NEG)

        def one_head(h, carry):
            col = column(h)
            own_k, own_v = sk_ref[:, col], with_ones(sv_ref[:, col])
            work = [(r, cell(r, half, h * group + i)) for r in range(2) for i in range(group)]
            queries = [q_ref[at] for _, at in work]

            def scores(j):
                return scores_of(queries[j], own_k[:(work[j][0] + 1) * half])

            done, s = [], scores(0)
            for j, (r, at) in enumerate(work):
                following = scores(j + 1) if j + 1 < len(work) else None
                done.append(own_rest(s, own_v[:(r + 1) * half], mask_ref[...], r * half))
                s = following
            for (_, at), new in zip(work, done):
                for ref, value in zip(state, new):
                    ref[at] = value
            if per_owner:
                @pl.when(wants(sel_ref, me_ref[0], h, per_owner))
                def _():
                    at = pl.ds(pl.multiple_of(local_row(sel_ref, me_ref[0], h, per_owner) * rows, rows), rows)
                    add_chunk(q_ref, state, state, (k_ref[at, col], v_ref[at, col]), h, group, rows // 4)
            return carry

        lax.fori_loop(0, kv_heads, one_head, 0)

    return pl.pallas_call(
        body, out_shape=state_shapes(query), in_specs=[SMEM] * 2 + [VMEM] * 5, out_specs=[VMEM] * 3,
        scratch_shapes=[pltpu.VMEM((half, half), jnp.float32)],
        compiler_params=WIDE, cost_estimate=cost(rows, kv_heads * group, 2),
    )(me, sel, *map(in_hbm, (query, span_keys, span_values, keys, values)))


def more_chunks(me, sel, query, sources, state, group, kv_heads, blocks):
    rows, half = query.shape[0], query.shape[0] // 2
    arrays = [a for s in sources for a in s[0]]

    def body(me_ref, sel_ref, q_ref, *refs):
        refs, old, state = refs[:len(arrays)], refs[len(arrays):len(arrays) + 3], refs[len(arrays) + 3:]
        def one_head(h, carry):
            cols = column(h, group * HEAD)
            at = 0
            for i, source in enumerate(sources):
                mine = refs[at:at + len(source[0])]
                at += len(source[0])
                needed = source[1](me_ref[0], sel_ref, h)

                @pl.when(needed)
                def _():
                    kv = source[2](mine, me_ref[0], sel_ref, h)
                    add_chunk(q_ref, state if i else old, state, kv, h, group, rows // 4)

                if i == 0:
                    @pl.when(jnp.logical_not(needed))
                    def _():
                        for new, previous in zip(state, old):
                            new[:, cols] = previous[:, cols]
            return carry

        lax.fori_loop(0, kv_heads, one_head, 0)

    n = 3 + len(arrays)
    return pl.pallas_call(
        body, out_shape=state_shapes(query), in_specs=[SMEM] * 2 + [VMEM] * (n + 1), out_specs=[VMEM] * 3,
        compiler_params=PARAMS, cost_estimate=cost(rows, kv_heads * group, blocks),
    )(me, sel, *map(near_core, (query, *arrays, *state)))


def finish(me, sel, query, arrays, when, read, state, group, head, parts):
    rows = query.shape[0]
    tile = rows // 4
    first = head * group
    width = group * HEAD
    whole = len(parts) == query.shape[1] // width - 1

    def body(me_ref, sel_ref, q_ref, *refs):
        part_refs = refs[len(arrays) + 3:len(arrays) + 3 + len(parts)] if whole else ()
        refs, state, rest = refs[:len(arrays)], refs[len(arrays):len(arrays) + 3], refs[len(arrays) + 3 + len(part_refs):]
        o_ref = rest[0]
        buf = rest[1] if whole else o_ref
        copies = [pltpu.make_async_copy(part, o_ref.at[:, pl.ds(i * width, width)], rest[2].at[group + i])
                  for i, part in enumerate(part_refs)]
        for copy in copies:
            copy.start()

        def tiles(fn):
            own = []
            for i in range(group):
                for r in range(rows // tile):
                    acc, den = fn(cell(r, tile, first + i))
                    buf[cell(r, tile, i)] = (acc / den).astype(jnp.bfloat16)
                if whole:
                    own.append(pltpu.make_async_copy(
                        buf.at[:, pl.ds(i * HEAD, HEAD)], o_ref.at[:, pl.ds((first + i) * HEAD, HEAD)], rest[2].at[i]))
                    own[-1].start()
            for copy in own:
                copy.wait()

        needed = when(me_ref[0], sel_ref, head)

        @pl.when(needed)
        def _():
            k, v = read(refs, me_ref[0], sel_ref, head)
            v = with_ones(v)
            tiles(lambda at: chunk_tile(q_ref[at], k, v, state[0][at], state[1][at], state[2][at])[:2])

        @pl.when(jnp.logical_not(needed))
        def _():
            tiles(lambda at: (state[0][at], state[1][at]))

        for copy in copies:
            copy.wait()

    n = 4 + len(arrays) + (len(parts) if whole else 0)
    scratch = [pltpu.VMEM((rows, width), jnp.bfloat16), pltpu.SemaphoreType.DMA((group + len(parts),))]
    return pl.pallas_call(
        body,
        out_shape=jax.ShapeDtypeStruct(query.shape, jnp.bfloat16) if whole else pltpu.VMEM((rows, width), jnp.bfloat16),
        in_specs=[SMEM] * 2 + [VMEM] * n, out_specs=ANY if whole else VMEM, scratch_shapes=scratch if whole else [],
        compiler_params=PARAMS, cost_estimate=cost(rows, group, 1),
    )(me, sel, *map(near_core, (query, *arrays, *state, *(parts if whole else ()))))


def pick(me, sels, arrays, rows, jobs, place=near_core):
    n, k = len(sels), len(arrays)

    def body(me_ref, *refs):
        sel_refs, refs, outs = refs[:n], refs[n:n + k], refs[n + k:]
        for out, parts in zip(outs, jobs):
            for when, keys, values, row, h, slot in parts:
                def copy():
                    at = pl.ds(pl.multiple_of(row(me_ref[0], sel_refs, h) * rows, rows), rows)
                    col = slice(h * HEAD, (h + 1) * HEAD)
                    out[2 * slot * rows:(2 * slot + 1) * rows] = refs[keys][at, col]
                    out[(2 * slot + 1) * rows:(2 * slot + 2) * rows] = refs[values][at, col]
                if when is None:
                    copy()
                else:
                    pl.when(when(me_ref[0]))(copy)

    shapes = [pltpu.VMEM((2 * rows * (1 + max(p[5] for p in parts)), HEAD), jnp.bfloat16) for parts in jobs]
    return pl.pallas_call(
        body, out_shape=shapes, in_specs=[SMEM] * (1 + n) + [VMEM] * k, out_specs=[VMEM] * len(jobs),
        compiler_params=PARAMS,
        cost_estimate=pl.CostEstimate(flops=0, transcendentals=0, bytes_accessed=8 * rows * HEAD * len(jobs)),
    )(me, *sels, *map(place, arrays))


def gathered(query, span_keys, span_values, cache_keys, stored_values, selected, group):
    rows = query.shape[0]
    kv_heads = span_keys.shape[1] // HEAD
    me = lax.axis_index("ctx").astype(jnp.int32).reshape(1)
    keys = lax.all_gather(cache_keys, "ctx", axis=0, tiled=True)
    values = lax.all_gather(stored_values, "ctx", axis=0, tiled=True)
    state = own_and_local(me, selected, query, span_keys, span_values, cache_keys, stored_values, 0, group)

    def always(m, s, h):
        return m >= 0

    def chosen(array, h, slot):
        start = jnp.clip(selected[0, h, slot], 0, keys.shape[0] // rows - 1) * rows
        return lax.dynamic_slice(array, (start, h * HEAD), (rows, HEAD))

    def stacked(refs, m, s, h):
        start = pl.multiple_of(2 * h * rows, rows)
        return refs[0][pl.ds(start, rows)], refs[0][pl.ds(start + rows, rows)]

    blocks = [[jnp.concatenate([chosen(a, h, slot) for h in range(kv_heads) for a in (keys, values)])] for slot in range(2)]
    state = more_chunks(me, selected, query, [(blocks[0], always, stacked)], state, group, kv_heads, 1)
    parts = []
    for h in range(kv_heads):
        parts.append(finish(me, selected, query, blocks[1], always, stacked, state, group, h, parts))
    return parts[-1]


def line_of_four(query, span_keys, span_values, cache_keys, stored_values, selected, group):
    rows = query.shape[0]
    kv_heads = span_keys.shape[1] // HEAD
    per_owner = cache_keys.shape[0] // rows
    me = lax.axis_index("ctx").astype(jnp.int32).reshape(1)
    heads = range(kv_heads)

    def inner(m):
        return (m == 1) | (m == 2)

    def outer(m):
        return (m == 0) | (m == 3)

    sel1 = lax.ppermute(selected, "ctx", [(0, 1), (1, 0), (2, 3), (3, 2)])
    mid_keys = lax.ppermute(cache_keys, "ctx", [(1, 2), (2, 1)])
    mid_values = lax.ppermute(stored_values, "ctx", [(1, 2), (2, 1)])
    both = lax.ppermute(jnp.concatenate([selected, sel1], axis=0), "ctx", [(3, 0), (0, 3)])

    out = pick(
        me, (sel1, both), (cache_keys, stored_values), rows,
        [[(None, 0, 1, lambda m, s, h: local_row(s[0], m, h, per_owner), h, 0)] for h in heads] +
        [[(outer, 0, 1, lambda m, s, h: local_row(s[1], m, h, per_owner), h, 0)] for h in heads], in_hbm)
    near_out, far_out = out[:kv_heads], out[kv_heads:]
    near = [lax.ppermute(n, "ctx", [(0, 1), (1, 0), (2, 3), (3, 2)]) for n in near_out]
    far = [lax.ppermute(f, "ctx", [(0, 3), (3, 0)]) for f in far_out[:-1]]

    near_out, far_out, span_keys = lax.optimization_barrier((near_out, far_out, span_keys))
    state = own_and_local(me, selected, query, span_keys, span_values, cache_keys, stored_values, per_owner, group)
    far_last, state = lax.optimization_barrier((far_out[-1], state))
    last = lax.ppermute(far_last, "ctx", [(0, 3), (3, 0)])
    far_last, state = lax.optimization_barrier((far_last, state))

    def single(refs, m, s, h):
        return refs[0][:rows], refs[0][rows:]

    near, far, state = lax.optimization_barrier((near, far, state))

    def stack(refs, m, s, h):
        k, v = refs[0][:rows], refs[0][rows:]
        for i in range(1, len(refs)):
            k, v = jnp.where(h == i, refs[i][:rows], k), jnp.where(h == i, refs[i][rows:], v)
        return k, v

    state = more_chunks(
        me, selected, query,
        [(tuple(near), lambda m, s, h: wants(s, m ^ 1, h, per_owner) & jnp.logical_not(wants(s, m, h, per_owner)), stack),
         (tuple(far), lambda m, s, h: outer(m) & (h < kv_heads - 1) & wants(s, m ^ 3, h, per_owner)
          & wants(s, m ^ 2, h, per_owner), stack)],
        state, group, kv_heads, 1)

    mid_keys, mid_values, state = lax.optimization_barrier((mid_keys, mid_values, state))
    cross_out = pick(
        me, (sel1, both), (cache_keys, stored_values, mid_keys, mid_values), rows,
        [[(inner, 2, 3, lambda m, s, h: local_row(s[0], m ^ 3, h, per_owner), h, 0),
          (outer, 0, 1, lambda m, s, h: local_row(s[1], m, h, per_owner, 1), h, 0)] for h in heads])
    cross = [lax.ppermute(c, "ctx", [(0, 2), (3, 1), (1, 0), (2, 3)]) for c in cross_out]

    def stacked(refs, m, s, h):
        start = pl.multiple_of(2 * h * rows, rows)
        return refs[0][pl.ds(start, rows)], refs[0][pl.ds(start + rows, rows)]

    def middle(refs, m, s, h):
        at = pl.ds(pl.multiple_of(local_row(s, m ^ 3, h, per_owner) * rows, rows), rows)
        return refs[0][at, column(h)], refs[1][at, column(h)]

    last, cross_out, state = lax.optimization_barrier((last, cross_out, state))
    state = more_chunks(
        me, selected, query,
        [((mid_keys, mid_values), lambda m, s, h: inner(m) & wants(s, m ^ 3, h, per_owner), middle),
         ((*far, last), lambda m, s, h: outer(m) & wants(s, m ^ 3, h, per_owner)
          & ((h == kv_heads - 1) | jnp.logical_not(wants(s, m ^ 2, h, per_owner))), stack),
         (tuple(near), lambda m, s, h: wants(s, m ^ 1, h, per_owner) & wants(s, m, h, per_owner), stack)],
        state, group, kv_heads, 1)
    parts = []
    for h in heads:
        parts.append(finish(me, selected, query, (cross[h],), lambda m, s, h: wants(s, m ^ 2, h, per_owner),
                            single, state, group, h, parts))
    return parts[-1]


def solution(mesh):
    kv = P(("groups", "ctx"), "mp")
    plan = line_of_four if mesh.shape["ctx"] == 4 else gathered

    def per_device(query, span_keys, span_values, cache_keys, stored_values, selected):
        group = query.shape[1] // span_keys.shape[1]
        return plan(query, span_keys, span_values, cache_keys, stored_values, selected, group)

    return jax.shard_map(
        per_device, mesh=mesh, in_specs=(kv, kv, kv, kv, kv, P(("groups", "ctx"), "mp", None)),
        out_specs=kv, check_vma=False)
```
